32 devices in a mesh: ctx: 8 (over z, y), tp: 4 (over x, core).
Axes of the slice: x: 2, y: 2, z: 4, core: 2. Of those that a mesh axis runs over, the one named last changes fastest.
Arguments:
- queries: bfloat16 [8192, 8192], P('ctx', 'tp'), may hold values from -170 to 170
- key_vectors: bfloat16 [8192, 8192], P('ctx', 'tp'), may hold values from -5 to 5
- value_vectors: bfloat16 [8192, 8192], P('ctx', 'tp'), may hold values from -5 to 5
- gate_logits: bfloat16 [8192, 8192], P('ctx', 'tp'), may hold values from -6 to 6
- norm_gain: float32 [8192], P('tp'), may hold values from 0.1 to 1.9
Outputs:
- attention_out: bfloat16 [8192, 8192], P('ctx', 'tp')
The draws below stay inside these ranges and needn't reach their ends.
All inputs are finite; a program needn't handle non-finite values.
Results may differ from the reference program's by a relative error of at most 0.0028.
Values sent between devices are 32-bit elements; how exact they have to be, the bound alone decides.
A program may use at most 128 MiB of HBM per device.

```python
import jax
import jax.numpy as jnp
from jax import lax

HEADS = 64
HEAD_DIM = 128
SLAB = 1024
TOKENS = 8192
N_CTX = 8


def draw_queries(key, part):
    first, second = jax.random.split(key)
    total_rows = TOKENS
    columns = HEADS * HEAD_DIM
    base = jnp.clip(jax.random.normal(first, (total_rows, columns), jnp.float32), -4.0, 4.0)
    rowscale = jnp.exp(jax.random.uniform(second, (total_rows, 1), jnp.float32) * jnp.log(10.0))
    ramp_top = jnp.log(4.0)
    head_index = (jnp.arange(columns) // HEAD_DIM).astype(jnp.float32)
    head_scale = jnp.exp(ramp_top * head_index / max(HEADS - 1, 1))
    return (base * rowscale * head_scale[None, :]).astype(jnp.bfloat16)


def levels(key, extent, pieces, smallest, top_value):
    gain, own = 1.0, jax.random.fold_in(key, 6)
    for axis_at, shards_of in pieces:
        heights = jnp.exp(jax.random.uniform(jax.random.fold_in(own, axis_at), (shards_of,), jnp.float32, smallest / len(pieces), top_value / len(pieces)))
        gain = gain * jnp.repeat(heights, extent[axis_at] // shards_of).reshape([-1 if axis == axis_at else 1 for axis in range(len(extent))])
    return gain


def scatter_about(own_key, extent, width, reach, cuts=(), kind=jnp.bfloat16):
    values = jax.random.normal(own_key, extent, jnp.float32) * width
    if len(cuts) > 0:
        values = levels(own_key, extent, cuts, -0.22, 0.18) * values
    return jnp.clip(values, min=-reach, max=reach).astype(kind)


def setup_inputs(seed: int = 0) -> dict:
    key_list = jax.random.split(jax.random.key(seed), 6)
    return {
        "queries": draw_queries(jax.random.fold_in(key_list[5], 71), 0),
        "key_vectors": scatter_about(key_list[1], (TOKENS, HEADS * HEAD_DIM), 1.0, 5.0, ((0, 8), (1, 4))),
        "value_vectors": scatter_about(key_list[2], (TOKENS, HEADS * HEAD_DIM), 1.0, 5.0, ((0, 8), (1, 4))),
        "gate_logits": scatter_about(key_list[3], (TOKENS, HEADS * HEAD_DIM), 1.5, 6.0, ((0, 8), (1, 4))),
        "norm_gain": jnp.clip(1.0 + 0.18 * jax.random.normal(key_list[4], (HEADS * HEAD_DIM,), jnp.float32), 0.1, 1.9),
    }


def reference(queries, key_vectors, value_vectors, gate_logits, norm_gain):
    shape = (N_CTX, SLAB, HEADS, HEAD_DIM)
    q_all = queries.reshape(shape)
    k_all = key_vectors.reshape(shape)
    v_all = value_vectors.reshape(shape)
    g_all = gate_logits.reshape(N_CTX, SLAB, HEADS * HEAD_DIM)
    places = jnp.arange(SLAB)
    causal = places[:, None] >= places[None, :]

    def slab_step(prefix, block):
        q_blk, k_blk, v_blk, g_blk = block
        q_f = q_blk.astype(jnp.float32)
        k_f = k_blk.astype(jnp.float32)
        v_f = v_blk.astype(jnp.float32)
        state = jnp.einsum('shd,she->hde', k_f, v_f)
        scores = jnp.einsum('qhd,khd->hqk', q_f, k_f)
        scores = jnp.where(causal[None], scores, 0.0).astype(jnp.bfloat16)
        intra = jnp.einsum('hqk,khd->qhd', scores.astype(jnp.float32), v_f)
        inter = jnp.einsum('qhd,hde->qhe', q_f, prefix, precision=lax.Precision.HIGHEST)
        attn = (intra + inter).reshape(SLAB, HEADS * HEAD_DIM)
        mean_square = lax.optimization_barrier(jnp.mean(attn * attn, axis=1, keepdims=True))
        result = attn * lax.rsqrt(mean_square + 1e-05) * norm_gain[None, :] * jax.nn.sigmoid(g_blk.astype(jnp.float32))
        return (prefix + state, result.astype(jnp.bfloat16))
    start = jnp.zeros((HEADS, HEAD_DIM, HEAD_DIM), jnp.float32)
    final, outputs = lax.scan(slab_step, start, (q_all, k_all, v_all, g_all))
    return outputs.reshape(TOKENS, HEADS * HEAD_DIM)
```

```python
import functools

import jax
import jax.numpy as jnp
from jax import lax
from jax.experimental import pallas as pl
from jax.experimental.pallas import tpu as pltpu
from jax.sharding import PartitionSpec as P

HEAD_DIM = 128
BLOCK = 256
STEPS_PER_HOP = 3
LAG = 3
MESH = pl.DeviceIdType.MESH


def columns_of(n_ctx):
    ny = 1
    while 2 * (2 * ny) * (2 * ny) <= n_ctx:
        ny *= 2
    return ny


def attention_kernel(
    n_ctx, n_tp,
    q_hbm, k_hbm, v_hbm, g_hbm, gain_ref,
    gated_hbm, scale_ref,
    q_buf, k_buf, v_buf, g_buf, attn, state,
    z_in, z_out, f_in, f_out, b_in, b_out,
    squares, sums, sums_in,
    load_sem, store_sem, z_send, z_recv, f_send, f_recv, b_send, b_recv, s_send, s_recv,
):
    heads, rows, _ = q_buf.shape
    ny = columns_of(n_ctx)
    nz = n_ctx // ny
    ctx = lax.axis_index("ctx")
    tp = lax.axis_index("tp")
    z = ctx // ny
    y = lax.rem(ctx, ny)

    def load(which, hbm, buf, h):
        return pltpu.make_async_copy(
            hbm.at[:, pl.ds(pl.multiple_of(h * HEAD_DIM, HEAD_DIM), HEAD_DIM)],
            buf.at[h], load_sem.at[which, h])

    def store(h):
        return pltpu.make_async_copy(
            attn.at[h],
            gated_hbm.at[:, pl.ds(pl.multiple_of(h * HEAD_DIM, HEAD_DIM), HEAD_DIM)],
            store_sem.at[h])

    def send(src, dst, ssem, rsem, h, to):
        return pltpu.make_async_remote_copy(
            src_ref=src.at[h], dst_ref=dst.at[h], send_sem=ssem.at[h], recv_sem=rsem.at[h],
            device_id=(to, tp), device_id_type=MESH)

    z_copy = lambda h: send(z_out, z_in, z_send, z_recv, h, jnp.minimum(ctx + ny, n_ctx - 1))
    f_copy = lambda h: send(f_out, f_in, f_send, f_recv, h, jnp.minimum(ctx + 1, n_ctx - 1))
    b_copy = lambda h: send(b_out, b_in, b_send, b_recv, h, jnp.maximum(ctx - 1, 0))

    def sum_copy(d):
        return pltpu.make_async_remote_copy(
            src_ref=sums, dst_ref=sums_in.at[d - 1], send_sem=s_send.at[d - 1],
            recv_sem=s_recv.at[d - 1], device_id=(ctx, lax.rem(tp + d, n_tp)),
            device_id_type=MESH)

    @pl.loop(0, heads)
    def _(h):
        load(0, k_hbm, k_buf, h).start()
        load(1, v_hbm, v_buf, h).start()

    @pl.loop(0, heads)
    def _(h):
        load(2, q_hbm, q_buf, h).start()
        load(3, g_hbm, g_buf, h).start()

    up, down, right, left = z < nz - 1, z > 0, y < ny - 1, y > 0
    barrier = pltpu.get_barrier_semaphore()
    for there, step in ((up, ny), (down, -ny), (right, 1), (left, -1)):
        @pl.when(there)
        def _():
            pl.semaphore_signal(barrier, inc=1, device_id=(ctx + step, tp), device_id_type=MESH)
    for d in range(1, n_tp):
        pl.semaphore_signal(
            barrier, inc=1, device_id=(ctx, lax.rem(tp + d, n_tp)), device_id_type=MESH)
    greeted = n_tp - 1
    for there in (up, down, right, left):
        greeted = greeted + jnp.where(there, 1, 0)
    pl.semaphore_wait(barrier, greeted)

    squares[...] = jnp.zeros_like(squares)

    def relay(h):
        @pl.when(down)
        def _():
            z_copy(h).wait_recv()

        @pl.when(z == 0)
        def _():
            z_in[h] = jnp.zeros((HEAD_DIM, HEAD_DIM), jnp.float32)

        before = z_in[h]
        after = before + state[h]

        @pl.when(up)
        def _():
            z_out[h] = after
            z_copy(h).start()

        @pl.when(jnp.logical_and(right, y == 0))
        def _():
            f_out[h] = after
            f_copy(h).start()

        @pl.when(jnp.logical_and(left, y == ny - 1))
        def _():
            b_out[h] = before
            b_copy(h).start()

    def finalize(h):
        prefix_in = z_in[h]
        zeros = jnp.zeros((HEAD_DIM, HEAD_DIM), jnp.float32)

        @pl.when(left)
        def _():
            f_copy(h).wait_recv()

            @pl.when(right)
            def _():
                f_out[h] = f_in[h] + (prefix_in + state[h])
                f_copy(h).start()

        @pl.when(y == 0)
        def _():
            f_in[h] = zeros

        @pl.when(right)
        def _():
            b_copy(h).wait_recv()

            @pl.when(left)
            def _():
                b_out[h] = b_in[h] + prefix_in
                b_copy(h).start()

        @pl.when(y == ny - 1)
        def _():
            b_in[h] = zeros

        prefix = prefix_in + f_in[h] + b_in[h]
        high = prefix.astype(jnp.bfloat16)
        low = (prefix - high.astype(jnp.float32)).astype(jnp.bfloat16)
        both = jnp.concatenate([high, low], axis=1)
        load(3, g_hbm, g_buf, h).wait()
        gain = gain_ref[h]
        for i in range(rows // BLOCK):
            here = pl.ds(i * BLOCK, BLOCK)
            inter = jnp.dot(q_buf[h, here, :], both, preferred_element_type=jnp.float32)
            total = attn[h, here, :] + (inter[:, :HEAD_DIM] + inter[:, HEAD_DIM:])
            squares[here, :] += total * total
            gate = jax.nn.sigmoid(g_buf[h, here, :].astype(jnp.float32))
            attn[h, here, :] = total * gain * gate
        store(h).start()

    def intra(h):
        load(2, q_hbm, q_buf, h).wait()
        row = lax.broadcasted_iota(jnp.int32, (BLOCK, BLOCK), 0)
        column = lax.broadcasted_iota(jnp.int32, (BLOCK, BLOCK), 1)
        for i in range(rows // BLOCK):
            here = pl.ds(i * BLOCK, BLOCK)
            q = q_buf[h, here, :]
            own = lax.dot_general(
                q, k_buf[h, here, :], (((1,), (1,)), ((), ())), preferred_element_type=jnp.float32)
            own = jnp.where(row >= column, own, 0.0).astype(jnp.bfloat16)
            out = jnp.dot(own, v_buf[h, here, :], preferred_element_type=jnp.float32)
            if i > 0:
                past = pl.ds(0, i * BLOCK)
                scores = lax.dot_general(
                    q, k_buf[h, past, :], (((1,), (1,)), ((), ())),
                    preferred_element_type=jnp.float32).astype(jnp.bfloat16)
                out += jnp.dot(scores, v_buf[h, past, :], preferred_element_type=jnp.float32)
            attn[h, here, :] = out

    @pl.loop(0, heads)
    def _(h):
        load(0, k_hbm, k_buf, h).wait()
        load(1, v_hbm, v_buf, h).wait()
        state[h] = lax.dot_general(
            k_buf[h], v_buf[h], (((0,), (0,)), ((), ())), preferred_element_type=jnp.float32)

        @pl.when(z == 0)
        def _():
            relay(h)

    delay = z * STEPS_PER_HOP

    @pl.loop(0, heads + delay + LAG)
    def _(s):
        @pl.when(jnp.logical_and(z > 0, jnp.logical_and(s >= delay, s < delay + heads)))
        def _():
            relay(s - delay)

        @pl.when(s < heads)
        def _():
            intra(s)

        @pl.when(s >= delay + LAG)
        def _():
            finalize(s - delay - LAG)

    sums[...] = jnp.sum(jnp.transpose(squares[...]), axis=0, keepdims=True)
    for d in range(1, n_tp):
        sum_copy(d).start()
    total = sums[...]
    for d in range(1, n_tp):
        sum_copy(d).wait_recv()
        total = total + sums_in[d - 1]
    mean_square = total / (heads * HEAD_DIM * n_tp)
    scale = lax.rsqrt(mean_square + 1e-05)
    scale_ref[...] = jnp.transpose(jnp.broadcast_to(scale, (HEAD_DIM, rows)))

    for d in range(1, n_tp):
        sum_copy(d).wait_send()

    @pl.loop(0, heads)
    def _(h):
        store(h).wait()

        @pl.when(up)
        def _():
            z_copy(h).wait_send()

        @pl.when(right)
        def _():
            f_copy(h).wait_send()

        @pl.when(left)
        def _():
            b_copy(h).wait_send()


def norm_kernel(gated_ref, scale_ref, out_ref):
    scale = scale_ref[...]
    for h in range(gated_ref.shape[1] // HEAD_DIM):
        here = pl.ds(h * HEAD_DIM, HEAD_DIM)
        out_ref[:, here] = (gated_ref[:, here] * scale).astype(out_ref.dtype)


def on_device(n_ctx, n_tp, queries, key_vectors, value_vectors, gate_logits, norm_gain):
    rows, width = queries.shape
    heads = width // HEAD_DIM
    head_array = lambda dtype: pltpu.VMEM((heads, rows, HEAD_DIM), dtype)
    states = pltpu.VMEM((heads, HEAD_DIM, HEAD_DIM), jnp.float32)
    dma = pltpu.SemaphoreType.DMA
    hbm = pl.BlockSpec(memory_space=pl.ANY)
    vmem = pl.BlockSpec(memory_space=pltpu.VMEM)
    gated, scale = pl.pallas_call(
        functools.partial(attention_kernel, n_ctx, n_tp),
        out_shape=(
            jax.ShapeDtypeStruct((rows, width), jnp.float32),
            jax.ShapeDtypeStruct((rows, HEAD_DIM), jnp.float32),
        ),
        in_specs=[hbm, hbm, hbm, hbm, vmem],
        out_specs=(hbm, vmem),
        scratch_shapes=[
            head_array(jnp.bfloat16), head_array(jnp.bfloat16), head_array(jnp.bfloat16),
            head_array(jnp.bfloat16), head_array(jnp.float32),
            states, states, states, states, states, states, states,
            pltpu.VMEM((rows, HEAD_DIM), jnp.float32),
            pltpu.VMEM((1, rows), jnp.float32),
            pltpu.VMEM((n_tp - 1, 1, rows), jnp.float32),
            dma((4, heads)), dma((heads,)),
            dma((heads,)), dma((heads,)), dma((heads,)), dma((heads,)), dma((heads,)), dma((heads,)),
            dma((n_tp - 1,)), dma((n_tp - 1,)),
        ],
        compiler_params=pltpu.CompilerParams(
            collective_id=0, has_side_effects=True, vmem_limit_bytes=48 * 1024 * 1024),
        name="attention",
    )(queries, key_vectors, value_vectors, gate_logits, norm_gain.reshape(heads, 1, HEAD_DIM))
    tile = min(rows, 128)
    return pl.pallas_call(
        norm_kernel,
        grid=(rows // tile,),
        out_shape=jax.ShapeDtypeStruct((rows, width), jnp.bfloat16),
        in_specs=[
            pl.BlockSpec((tile, width), lambda i: (i, 0)),
            pl.BlockSpec((tile, HEAD_DIM), lambda i: (i, 0)),
        ],
        out_specs=pl.BlockSpec((tile, width), lambda i: (i, 0)),
        name="norm",
    )(gated, scale)


def solution(mesh):
    return jax.shard_map(
        functools.partial(on_device, mesh.shape["ctx"], mesh.shape["tp"]),
        mesh=mesh,
        in_specs=(P("ctx", "tp"), P("ctx", "tp"), P("ctx", "tp"), P("ctx", "tp"), P("tp")),
        out_specs=P("ctx", "tp"),
        check_vma=False,
    )
```

```python
import functools

import jax
import jax.numpy as jnp
from jax import lax
from jax.experimental import pallas as pl
from jax.experimental.pallas import tpu as pltpu
from jax.sharding import PartitionSpec as P

HEAD_DIM = 128
BLOCK = 256
STEPS_PER_HOP = 3
LAG = 3
NORM_ROWS = 128
MESH = pl.DeviceIdType.MESH


def columns_of(n_ctx):
    ny = 1
    while 2 * (2 * ny) * (2 * ny) <= n_ctx:
        ny *= 2
    return ny


def attention_kernel(
    n_ctx, n_tp,
    q_hbm, k_hbm, v_hbm, g_hbm, gain_hbm,
    attn, scale_ref,
    q_buf, k_buf, v_buf, g_buf, gain_ref, states,
    z_in, z_out, f_in, f_out, b_in, b_out,
    squares, sums, sums_in,
    load_sem, gain_sem, z_send, z_recv, f_send, f_recv, b_send, b_recv, s_send, s_recv,
):
    heads, rows, _ = q_buf.shape
    blocks = rows // BLOCK
    ny = columns_of(n_ctx)
    nz = n_ctx // ny
    ctx = lax.axis_index("ctx")
    tp = lax.axis_index("tp")
    z = ctx // ny
    y = lax.rem(ctx, ny)

    def load(which, hbm, buf, h):
        return pltpu.make_async_copy(
            hbm.at[:, pl.ds(pl.multiple_of(h * HEAD_DIM, HEAD_DIM), HEAD_DIM)],
            buf.at[h], load_sem.at[which, h])

    def send(src, dst, ssem, rsem, h, to):
        return pltpu.make_async_remote_copy(
            src_ref=src.at[h], dst_ref=dst.at[h], send_sem=ssem.at[h], recv_sem=rsem.at[h],
            device_id=(to, tp), device_id_type=MESH)

    z_copy = lambda h: send(z_out, z_in, z_send, z_recv, h, jnp.minimum(ctx + ny, n_ctx - 1))
    f_copy = lambda h: send(f_out, f_in, f_send, f_recv, h, jnp.minimum(ctx + 1, n_ctx - 1))
    b_copy = lambda h: send(b_out, b_in, b_send, b_recv, h, jnp.maximum(ctx - 1, 0))

    def sum_copy(d):
        return pltpu.make_async_remote_copy(
            src_ref=sums, dst_ref=sums_in.at[d - 1], send_sem=s_send.at[d - 1],
            recv_sem=s_recv.at[d - 1], device_id=(ctx, lax.rem(tp + d, n_tp)),
            device_id_type=MESH)

    @pl.loop(0, heads)
    def _(h):
        load(0, k_hbm, k_buf, h).start()
        load(1, v_hbm, v_buf, h).start()

    @pl.loop(0, heads)
    def _(h):
        load(2, q_hbm, q_buf, h).start()
        load(3, g_hbm, g_buf, h).start()

    pltpu.make_async_copy(gain_hbm, gain_ref, gain_sem).start()

    up, down, right, left = z < nz - 1, z > 0, y < ny - 1, y > 0
    barrier = pltpu.get_barrier_semaphore()
    for there, step in ((up, ny), (down, -ny), (right, 1), (left, -1)):
        @pl.when(there)
        def _():
            pl.semaphore_signal(barrier, inc=1, device_id=(ctx + step, tp), device_id_type=MESH)
    for d in range(1, n_tp):
        pl.semaphore_signal(
            barrier, inc=1, device_id=(ctx, lax.rem(tp + d, n_tp)), device_id_type=MESH)
    greeted = n_tp - 1
    for there in (up, down, right, left):
        greeted = greeted + jnp.where(there, 1, 0)
    pl.semaphore_wait(barrier, greeted)

    squares[...] = jnp.zeros_like(squares)

    def relay(h):
        @pl.when(down)
        def _():
            z_copy(h).wait_recv()

        @pl.when(z == 0)
        def _():
            z_in[h] = jnp.zeros((HEAD_DIM, HEAD_DIM), jnp.float32)

        before = z_in[h]
        after = before + states[h, blocks - 1]

        @pl.when(up)
        def _():
            z_out[h] = after
            z_copy(h).start()

        @pl.when(jnp.logical_and(right, y == 0))
        def _():
            f_out[h] = after
            f_copy(h).start()

        @pl.when(jnp.logical_and(left, y == ny - 1))
        def _():
            b_out[h] = before
            b_copy(h).start()

    def finalize(h):
        prefix_in = z_in[h]
        zeros = jnp.zeros((HEAD_DIM, HEAD_DIM), jnp.float32)

        @pl.when(left)
        def _():
            f_copy(h).wait_recv()

            @pl.when(right)
            def _():
                f_out[h] = f_in[h] + (prefix_in + states[h, blocks - 1])
                f_copy(h).start()

        @pl.when(y == 0)
        def _():
            f_in[h] = zeros

        @pl.when(right)
        def _():
            b_copy(h).wait_recv()

            @pl.when(left)
            def _():
                b_out[h] = b_in[h] + prefix_in
                b_copy(h).start()

        @pl.when(y == ny - 1)
        def _():
            b_in[h] = zeros

        prefix = prefix_in + f_in[h] + b_in[h]
        load(3, g_hbm, g_buf, h).wait()
        gain = gain_ref[h]
        for i in range(blocks):
            here = pl.ds(i * BLOCK, BLOCK)
            before = prefix if i == 0 else prefix + states[h, i - 1]
            high = before.astype(jnp.bfloat16)
            low = (before - high.astype(jnp.float32)).astype(jnp.bfloat16)
            both = jnp.concatenate([high, low], axis=1)
            inter = jnp.dot(q_buf[h, here, :], both, preferred_element_type=jnp.float32)
            total = attn[h, here, :] + (inter[:, :HEAD_DIM] + inter[:, HEAD_DIM:])
            squares[here, :] += total * total
            gate = 0.5 + 0.5 * jnp.tanh(0.5 * g_buf[h, here, :].astype(jnp.float32))
            attn[h, here, :] = total * gain * gate

    def intra(h):
        load(2, q_hbm, q_buf, h).wait()
        row = lax.broadcasted_iota(jnp.int32, (BLOCK, BLOCK), 0)
        column = lax.broadcasted_iota(jnp.int32, (BLOCK, BLOCK), 1)
        for i in range(blocks):
            here = pl.ds(i * BLOCK, BLOCK)
            q = q_buf[h, here, :]
            own = lax.dot_general(
                q, k_buf[h, here, :], (((1,), (1,)), ((), ())), preferred_element_type=jnp.float32)
            own = jnp.where(row >= column, own, 0.0).astype(jnp.bfloat16)
            attn[h, here, :] = jnp.dot(own, v_buf[h, here, :], preferred_element_type=jnp.float32)

    @pl.loop(0, heads)
    def _(h):
        load(0, k_hbm, k_buf, h).wait()
        load(1, v_hbm, v_buf, h).wait()
        running = None
        for i in range(blocks):
            here = pl.ds(i * BLOCK, BLOCK)
            own = lax.dot_general(
                k_buf[h, here, :], v_buf[h, here, :], (((0,), (0,)), ((), ())),
                preferred_element_type=jnp.float32)
            running = own if i == 0 else running + own
            states[h, i] = running

        @pl.when(z == 0)
        def _():
            relay(h)

    pltpu.make_async_copy(gain_hbm, gain_ref, gain_sem).wait()
    delay = z * STEPS_PER_HOP

    @pl.loop(0, heads + delay + LAG)
    def _(s):
        @pl.when(jnp.logical_and(z > 0, jnp.logical_and(s >= delay, s < delay + heads)))
        def _():
            relay(s - delay)

        @pl.when(s < heads)
        def _():
            intra(s)

        @pl.when(s >= delay + LAG)
        def _():
            finalize(s - delay - LAG)

    sums[...] = jnp.sum(jnp.transpose(squares[...]), axis=0, keepdims=True)
    for d in range(1, n_tp):
        sum_copy(d).start()
    total = sums[...]
    for d in range(1, n_tp):
        sum_copy(d).wait_recv()
        total = total + sums_in[d - 1]
    mean_square = total / (heads * HEAD_DIM * n_tp)
    scale = lax.rsqrt(mean_square + 1e-05)
    scale_ref[...] = jnp.transpose(jnp.broadcast_to(scale, (HEAD_DIM, rows)))

    for d in range(1, n_tp):
        sum_copy(d).wait_send()

    @pl.loop(0, heads)
    def _(h):
        @pl.when(up)
        def _():
            z_copy(h).wait_send()

        @pl.when(right)
        def _():
            f_copy(h).wait_send()

        @pl.when(left)
        def _():
            b_copy(h).wait_send()


def norm_kernel(gated_ref, scale_ref, out_hbm, tiles, sems):
    heads, rows, _ = gated_ref.shape
    count = rows // NORM_ROWS

    def store(i):
        here = pl.ds(i * NORM_ROWS, NORM_ROWS)
        return pltpu.make_async_copy(tiles.at[here, :], out_hbm.at[here, :], sems.at[i])

    for i in range(count):
        here = pl.ds(i * NORM_ROWS, NORM_ROWS)
        scale = scale_ref[here, :]
        for h in range(heads):
            tiles[here, pl.ds(h * HEAD_DIM, HEAD_DIM)] = (
                gated_ref[h, here, :] * scale).astype(tiles.dtype)
        store(i).start()
    for i in range(count):
        store(i).wait()


def on_device(n_ctx, n_tp, queries, key_vectors, value_vectors, gate_logits, norm_gain):
    rows, width = queries.shape
    heads = width // HEAD_DIM
    head_array = lambda dtype: pltpu.VMEM((heads, rows, HEAD_DIM), dtype)
    states = pltpu.VMEM((heads, HEAD_DIM, HEAD_DIM), jnp.float32)
    dma = pltpu.SemaphoreType.DMA
    hbm = pl.BlockSpec(memory_space=pltpu.HBM)
    vmem = pl.BlockSpec(memory_space=pltpu.VMEM)
    gated, scale = pl.pallas_call(
        functools.partial(attention_kernel, n_ctx, n_tp),
        out_shape=(
            pltpu.VMEM((heads, rows, HEAD_DIM), jnp.float32),
            pltpu.VMEM((rows, HEAD_DIM), jnp.float32),
        ),
        in_specs=[hbm, hbm, hbm, hbm, hbm],
        out_specs=(vmem, vmem),
        scratch_shapes=[
            head_array(jnp.bfloat16), head_array(jnp.bfloat16), head_array(jnp.bfloat16),
            head_array(jnp.bfloat16), pltpu.VMEM((heads, 1, HEAD_DIM), jnp.float32),
            pltpu.VMEM((heads, rows // BLOCK, HEAD_DIM, HEAD_DIM), jnp.float32),
            states, states, states, states, states, states,
            pltpu.VMEM((rows, HEAD_DIM), jnp.float32),
            pltpu.VMEM((1, rows), jnp.float32),
            pltpu.VMEM((n_tp - 1, 1, rows), jnp.float32),
            dma((4, heads)), dma(()),
            dma((heads,)), dma((heads,)), dma((heads,)), dma((heads,)), dma((heads,)), dma((heads,)),
            dma((n_tp - 1,)), dma((n_tp - 1,)),
        ],
        compiler_params=pltpu.CompilerParams(
            collective_id=0, has_side_effects=True, vmem_limit_bytes=50 * 1024 * 1024),
        name="attention",
    )(queries, key_vectors, value_vectors, gate_logits, norm_gain.reshape(heads, 1, HEAD_DIM))
    return pl.pallas_call(
        norm_kernel,
        out_shape=jax.ShapeDtypeStruct((rows, width), jnp.bfloat16),
        in_specs=[vmem, vmem],
        out_specs=hbm,
        scratch_shapes=[pltpu.VMEM((rows, width), jnp.bfloat16), dma((rows // NORM_ROWS,))],
        compiler_params=pltpu.CompilerParams(vmem_limit_bytes=16 * 1024 * 1024),
        name="norm",
    )(gated, scale)


def solution(mesh):
    return jax.shard_map(
        functools.partial(on_device, mesh.shape["ctx"], mesh.shape["tp"]),
        mesh=mesh,
        in_specs=(P("ctx", "tp"), P("ctx", "tp"), P("ctx", "tp"), P("ctx", "tp"), P("tp")),
        out_specs=P("ctx", "tp"),
        check_vma=False,
    )
```

```python
import functools

import jax
import jax.numpy as jnp
from jax import lax
from jax.experimental import pallas as pl
from jax.experimental.pallas import tpu as pltpu
from jax.sharding import PartitionSpec as P

HEAD_DIM = 128
BLOCK = 256
STEPS_PER_HOP = 4
LAG = 3
FIRST_RELAY = 2
OWN_LAG = 4
NORM_ROWS = 128
MESH = pl.DeviceIdType.MESH


def columns_of(n_ctx):
    ny = 1
    while 2 * (2 * ny) * (2 * ny) <= n_ctx:
        ny *= 2
    return ny


def attention_kernel(
    n_ctx, n_tp,
    q_hbm, k_hbm, v_hbm, g_hbm, gain_hbm,
    attn, scale_ref,
    q_buf, k_buf, v_buf, g_buf, gain_ref, states,
    z_in, z_out, f_in, f_out, b_in, b_out,
    squares, sums, sums_in,
    load_sem, gain_sem, z_send, z_recv, f_send, f_recv, b_send, b_recv, s_send, s_recv,
):
    heads, rows, _ = q_buf.shape
    blocks = rows // BLOCK
    ny = columns_of(n_ctx)
    nz = n_ctx // ny
    ctx = lax.axis_index("ctx")
    tp = lax.axis_index("tp")
    z = ctx // ny
    y = lax.rem(ctx, ny)

    def load(which, hbm, buf, h):
        return pltpu.make_async_copy(
            hbm.at[:, pl.ds(pl.multiple_of(h * HEAD_DIM, HEAD_DIM), HEAD_DIM)],
            buf.at[h], load_sem.at[which, h])

    def send(src, dst, ssem, rsem, h, to):
        return pltpu.make_async_remote_copy(
            src_ref=src.at[h], dst_ref=dst.at[h], send_sem=ssem.at[h], recv_sem=rsem.at[h],
            device_id=(to, tp), device_id_type=MESH)

    z_copy = lambda h: send(z_out, z_in, z_send, z_recv, h, jnp.minimum(ctx + ny, n_ctx - 1))
    f_copy = lambda h: send(f_out, f_in, f_send, f_recv, h, jnp.minimum(ctx + 1, n_ctx - 1))
    b_copy = lambda h: send(b_out, b_in, b_send, b_recv, h, jnp.maximum(ctx - 1, 0))

    def sum_copy(d):
        return pltpu.make_async_remote_copy(
            src_ref=sums, dst_ref=sums_in.at[d - 1], send_sem=s_send.at[d - 1],
            recv_sem=s_recv.at[d - 1], device_id=(ctx, lax.rem(tp + d, n_tp)),
            device_id_type=MESH)

    first = heads // 2 * (1 - y) if ny == 2 else 0

    @pl.loop(0, heads)
    def _(i):
        h = lax.rem(i + first, heads)
        load(0, k_hbm, k_buf, h).start()
        load(1, v_hbm, v_buf, h).start()

    @pl.loop(0, heads)
    def _(i):
        h = lax.rem(i + first, heads)
        load(2, q_hbm, q_buf, h).start()
        load(3, g_hbm, g_buf, h).start()

    pltpu.make_async_copy(gain_hbm, gain_ref, gain_sem).start()

    up, down, right, left = z < nz - 1, z > 0, y < ny - 1, y > 0
    barrier = pltpu.get_barrier_semaphore()
    for there, step in ((up, ny), (down, -ny), (right, 1), (left, -1)):
        @pl.when(there)
        def _():
            pl.semaphore_signal(barrier, inc=1, device_id=(ctx + step, tp), device_id_type=MESH)
    for d in range(1, n_tp):
        pl.semaphore_signal(
            barrier, inc=1, device_id=(ctx, lax.rem(tp + d, n_tp)), device_id_type=MESH)
    greeted = n_tp - 1
    for there in (up, down, right, left):
        greeted = greeted + jnp.where(there, 1, 0)
    pl.semaphore_wait(barrier, greeted)

    squares[...] = jnp.zeros_like(squares)

    def relay(h):
        @pl.when(down)
        def _():
            z_copy(h).wait_recv()

        @pl.when(z == 0)
        def _():
            z_in[h] = jnp.zeros((HEAD_DIM, HEAD_DIM), jnp.float32)

        before = z_in[h]
        after = before + states[h, blocks - 1]

        @pl.when(up)
        def _():
            z_out[h] = after
            z_copy(h).start()

        @pl.when(jnp.logical_and(right, y == 0))
        def _():
            f_out[h] = after
            f_copy(h).start()

        @pl.when(jnp.logical_and(left, y == ny - 1))
        def _():
            b_out[h] = before
            b_copy(h).start()

    def finalize(h):
        prefix_in = z_in[h]
        zeros = jnp.zeros((HEAD_DIM, HEAD_DIM), jnp.float32)

        @pl.when(left)
        def _():
            f_copy(h).wait_recv()

            @pl.when(right)
            def _():
                f_out[h] = f_in[h] + (prefix_in + states[h, blocks - 1])
                f_copy(h).start()

        @pl.when(y == 0)
        def _():
            f_in[h] = zeros

        @pl.when(right)
        def _():
            b_copy(h).wait_recv()

            @pl.when(left)
            def _():
                b_out[h] = b_in[h] + prefix_in
                b_copy(h).start()

        @pl.when(y == ny - 1)
        def _():
            b_in[h] = zeros

        prefix = prefix_in + f_in[h] + b_in[h]
        apply_prefix(h, prefix)

    def apply_prefix(h, prefix):
        load(3, g_hbm, g_buf, h).wait()
        gain = gain_ref[h]
        for i in range(blocks):
            here = pl.ds(i * BLOCK, BLOCK)
            before = prefix if i == 0 else prefix + states[h, i - 1]
            high = before.astype(jnp.bfloat16)
            low = (before - high.astype(jnp.float32)).astype(jnp.bfloat16)
            both = jnp.concatenate([high, low], axis=1)
            inter = jnp.dot(q_buf[h, here, :], both, preferred_element_type=jnp.float32)
            total = attn[h, here, :] + (inter[:, :HEAD_DIM] + inter[:, HEAD_DIM:])
            squares[here, :] += total * total
            gate = 0.5 + 0.5 * jnp.tanh(0.5 * g_buf[h, here, :].astype(jnp.float32))
            attn[h, here, :] = total * gain * gate

    def intra(h):
        load(2, q_hbm, q_buf, h).wait()
        row = lax.broadcasted_iota(jnp.int32, (BLOCK, BLOCK), 0)
        column = lax.broadcasted_iota(jnp.int32, (BLOCK, BLOCK), 1)
        places = [pl.ds(i * BLOCK, BLOCK) for i in range(blocks)]
        scores = [
            lax.dot_general(
                q_buf[h, here, :], k_buf[h, here, :], (((1,), (1,)), ((), ())),
                preferred_element_type=jnp.float32)
            for here in places
        ]
        scores = [jnp.where(row >= column, own, 0.0).astype(jnp.bfloat16) for own in scores]
        outs = [
            jnp.dot(own, v_buf[h, here, :], preferred_element_type=jnp.float32)
            for own, here in zip(scores, places)
        ]
        for here, out in zip(places, outs):
            attn[h, here, :] = out

    def slab_state(h):
        load(0, k_hbm, k_buf, h).wait()
        load(1, v_hbm, v_buf, h).wait()
        running = None
        for i in range(blocks):
            here = pl.ds(i * BLOCK, BLOCK)
            own = lax.dot_general(
                k_buf[h, here, :], v_buf[h, here, :], (((0,), (0,)), ((), ())),
                preferred_element_type=jnp.float32)
            running = own if i == 0 else running + own
            states[h, i] = running

    def run_chains():
        @pl.loop(0, heads)
        def _(h):
            slab_state(h)

            @pl.when(z == 0)
            def _():
                relay(h)

        delay = z * STEPS_PER_HOP

        @pl.loop(0, heads + delay + LAG)
        def _(s):
            @pl.when(jnp.logical_and(z > 0, jnp.logical_and(s >= delay, s < delay + heads)))
            def _():
                relay(s - delay)

            @pl.when(s < heads)
            def _():
                intra(s)

            @pl.when(s >= delay + LAG)
            def _():
                finalize(s - delay - LAG)

        @pl.loop(0, heads)
        def _(h):
            @pl.when(up)
            def _():
                z_copy(h).wait_send()

            @pl.when(right)
            def _():
                f_copy(h).wait_send()

            @pl.when(left)
            def _():
                b_copy(h).wait_send()

    half = heads // 2
    mate = ctx + 1 - 2 * y

    def raw_copy(i):
        return pltpu.make_async_remote_copy(
            src_ref=states.at[(1 - y) * half + i, blocks - 1], dst_ref=f_in.at[i],
            send_sem=f_send.at[i], recv_sem=f_recv.at[i],
            device_id=(mate, tp), device_id_type=MESH)

    mate_copy = lambda i: send(b_out, b_in, b_send, b_recv, i, mate)

    def pair_relay(i):
        h = y * half + i
        raw_copy(i).wait_recv()

        @pl.when(down)
        def _():
            z_copy(i).wait_recv()

        @pl.when(z == 0)
        def _():
            z_in[i] = jnp.zeros((HEAD_DIM, HEAD_DIM), jnp.float32)

        before = z_in[i]
        mine = states[h, blocks - 1]

        @pl.when(up)
        def _():
            z_out[i] = before + (mine + f_in[i])
            z_copy(i).start()

        b_out[i] = before + jnp.where(y == 0, mine, 0.0)
        mate_copy(i).start()

    def run_pairs():
        @pl.loop(0, half)
        def _(i):
            slab_state((1 - y) * half + i)
            raw_copy(i).start()

        @pl.loop(0, half)
        def _(i):
            slab_state(y * half + i)

        delay = FIRST_RELAY + z * STEPS_PER_HOP

        @pl.loop(0, jnp.maximum(heads, delay + 2 * half))
        def _(s):
            at = s - delay

            @pl.when(jnp.logical_and(at >= 0, at < half))
            def _():
                pair_relay(at)

            @pl.when(s < heads)
            def _():
                intra(lax.rem(s + y * half, heads))

            @pl.when(jnp.logical_and(at >= OWN_LAG, at < half + OWN_LAG))
            def _():
                i = at - OWN_LAG
                apply_prefix(y * half + i, z_in[i] + jnp.where(y == 0, 0.0, f_in[i]))

            @pl.when(jnp.logical_and(at >= half, at < 2 * half))
            def _():
                i = at - half
                mate_copy(i).wait_recv()
                apply_prefix((1 - y) * half + i, b_in[i])

        @pl.loop(0, half)
        def _(i):
            raw_copy(i).wait_send()
            mate_copy(i).wait_send()

            @pl.when(up)
            def _():
                z_copy(i).wait_send()

    pltpu.make_async_copy(gain_hbm, gain_ref, gain_sem).wait()
    if ny == 2 and heads % 2 == 0:
        run_pairs()
    else:
        run_chains()

    sums[...] = jnp.sum(jnp.transpose(squares[...]), axis=0, keepdims=True)
    for d in range(1, n_tp):
        sum_copy(d).start()
    total = sums[...]
    for d in range(1, n_tp):
        sum_copy(d).wait_recv()
        total = total + sums_in[d - 1]
    mean_square = total / (heads * HEAD_DIM * n_tp)
    scale = lax.rsqrt(mean_square + 1e-05)
    scale_ref[...] = jnp.transpose(jnp.broadcast_to(scale, (HEAD_DIM, rows)))

    for d in range(1, n_tp):
        sum_copy(d).wait_send()


def norm_kernel(gated_ref, scale_ref, out_hbm, tiles, sems):
    heads, rows, _ = gated_ref.shape
    count = rows // NORM_ROWS

    def store(i):
        here = pl.ds(i * NORM_ROWS, NORM_ROWS)
        return pltpu.make_async_copy(tiles.at[here, :], out_hbm.at[here, :], sems.at[i])

    for i in range(count):
        here = pl.ds(i * NORM_ROWS, NORM_ROWS)
        scale = scale_ref[here, :]
        for h in range(heads):
            tiles[here, pl.ds(h * HEAD_DIM, HEAD_DIM)] = (
                gated_ref[h, here, :] * scale).astype(tiles.dtype)
        store(i).start()
    for i in range(count):
        store(i).wait()


def on_device(n_ctx, n_tp, queries, key_vectors, value_vectors, gate_logits, norm_gain):
    rows, width = queries.shape
    heads = width // HEAD_DIM
    head_array = lambda dtype: pltpu.VMEM((heads, rows, HEAD_DIM), dtype)
    states = pltpu.VMEM((heads, HEAD_DIM, HEAD_DIM), jnp.float32)
    dma = pltpu.SemaphoreType.DMA
    hbm = pl.BlockSpec(memory_space=pltpu.HBM)
    vmem = pl.BlockSpec(memory_space=pltpu.VMEM)
    gated, scale = pl.pallas_call(
        functools.partial(attention_kernel, n_ctx, n_tp),
        out_shape=(
            pltpu.VMEM((heads, rows, HEAD_DIM), jnp.float32),
            pltpu.VMEM((rows, HEAD_DIM), jnp.float32),
        ),
        in_specs=[hbm, hbm, hbm, hbm, hbm],
        out_specs=(vmem, vmem),
        scratch_shapes=[
            head_array(jnp.bfloat16), head_array(jnp.bfloat16), head_array(jnp.bfloat16),
            head_array(jnp.bfloat16), pltpu.VMEM((heads, 1, HEAD_DIM), jnp.float32),
            pltpu.VMEM((heads, rows // BLOCK, HEAD_DIM, HEAD_DIM), jnp.float32),
            states, states, states, states, states, states,
            pltpu.VMEM((rows, HEAD_DIM), jnp.float32),
            pltpu.VMEM((1, rows), jnp.float32),
            pltpu.VMEM((n_tp - 1, 1, rows), jnp.float32),
            dma((4, heads)), dma(()),
            dma((heads,)), dma((heads,)), dma((heads,)), dma((heads,)), dma((heads,)), dma((heads,)),
            dma((n_tp - 1,)), dma((n_tp - 1,)),
        ],
        compiler_params=pltpu.CompilerParams(
            collective_id=0, has_side_effects=True, vmem_limit_bytes=50 * 1024 * 1024),
        name="attention",
    )(queries, key_vectors, value_vectors, gate_logits, norm_gain.reshape(heads, 1, HEAD_DIM))
    return pl.pallas_call(
        norm_kernel,
        out_shape=jax.ShapeDtypeStruct((rows, width), jnp.bfloat16),
        in_specs=[vmem, vmem],
        out_specs=hbm,
        scratch_shapes=[pltpu.VMEM((rows, width), jnp.bfloat16), dma((rows // NORM_ROWS,))],
        compiler_params=pltpu.CompilerParams(vmem_limit_bytes=16 * 1024 * 1024),
        name="norm",
    )(gated, scale)


def solution(mesh):
    return jax.shard_map(
        functools.partial(on_device, mesh.shape["ctx"], mesh.shape["tp"]),
        mesh=mesh,
        in_specs=(P("ctx", "tp"), P("ctx", "tp"), P("ctx", "tp"), P("ctx", "tp"), P("tp")),
        out_specs=P("ctx", "tp"),
        check_vma=False,
    )
```
